128 devices in a mesh: grp: 4 (over z_hi, core), mem: 32 (over x, y, z_lo).
Axes of the slice: x: 4, y: 4, z: 4 (z_hi: 2, z_lo: 2; z = z_hi * 2 + z_lo), core: 2. Of those that a mesh axis runs over, the one named last changes fastest.
Arguments:
- amplitudes: bfloat16 [384, 1048576], P('mem', 'grp'), may hold values from -6 to 6
- integrals: bfloat16 [1048576, 1024], P(('grp', 'mem')), may hold values from -0.0625 to 0.0625
- irrep_ef: int32 [1048576], P(('grp', 'mem')), may hold values from 0 to 7
- irrep_ab: int32 [1024], replicated, may hold values from 0 to 7
Outputs:
- residual: float32 [384, 1024], P('mem', 'grp')
The draws below stay inside these ranges and needn't reach their ends.
All inputs are finite; a program needn't handle non-finite values.
Results may differ from the reference program's by a relative error of at most 0.0003.
Values may be sent and summed in bfloat16 or wider, within the bound.
A program may use at most 128 MiB of HBM per device.

```python
import jax
import jax.numpy as jnp
from jax import lax

OP = 384
EF_DEV = 8192
AB = 1024
EF = 1048576


def plant(result, key, smallest, largest):
    shape = result.shape
    place = [jax.random.randint(jax.random.fold_in(key, axis), (), 0, shape[axis]) for axis in range(len(shape))]
    result = result.at[tuple(place)].set(smallest)
    longest = shape.index(max(shape))
    place[longest] = (place[longest] + 1) % shape[longest]
    return result.at[tuple(place)].set(largest)


def raised(drawn, own_key, source, target, parts, factor):
    def block_of(dim):
        return (jnp.arange(drawn.shape[dim]) // (drawn.shape[dim] // parts)).reshape((-1,) + (1,) * (drawn.ndim - 1 - dim))

    near = jax.random.permutation(own_key, parts)[block_of(target)]
    other_side = (block_of(target) + parts // 2) % parts
    return jnp.where((block_of(source) == near) | (block_of(source) == other_side), factor * drawn, drawn)


def levels(stream_key, shape, shards, smallest, high):
    loudness, own = 1.0, jax.random.fold_in(stream_key, 6)
    for dim, shards_of in shards:
        draws = jnp.exp(jax.random.uniform(jax.random.fold_in(own, dim), (shards_of,), jnp.float32, smallest / len(shards), high / len(shards)))
        loudness = loudness * jnp.repeat(draws, shape[dim] // shards_of).reshape([-1 if axis == dim else 1 for axis in range(len(shape))])
    return loudness


def noise(own_key, dims, width, bound, split=(), held_as=jnp.bfloat16):
    gain = levels(own_key, dims, split, -0.22, 0.18) if split else 1.0
    entries = jax.random.normal(own_key, dims, jnp.float32) * width * gain
    return jnp.minimum(jnp.maximum(entries, -bound), bound).astype(held_as)


def gaussian_with(own_key, extent, width, most, pieces, heavy, kind=jnp.bfloat16):
    drawn = width * jax.random.normal(own_key, extent, jnp.float32)
    if pieces:
        drawn = drawn * levels(own_key, extent, pieces, -0.22, 0.18)
    return jnp.clip(raised(drawn, jax.random.fold_in(own_key, 3), *heavy), -most, most).astype(kind)


def setup_inputs(seed: int = 0) -> dict:
    streams_of = jax.random.split(jax.random.key(seed), 5)
    amplitudes = noise(streams_of[0], (OP, EF), 1.0, 6.0, ((0, 32), (1, 4)))
    integrals = gaussian_with(streams_of[1], (EF, AB), (EF // 8) ** -0.5, 0.0625, ((0, 128),), (0, 1, 128, 5.5))
    irrep_ef = plant(jax.random.randint(streams_of[2], (EF,), 0, 8), jax.random.fold_in(streams_of[2], 1), 0, 7).astype(jnp.int32)
    irrep_ab = plant(jax.random.randint(streams_of[3], (AB,), 0, 8), jax.random.fold_in(streams_of[3], 1), 0, 7).astype(jnp.int32)
    return dict(amplitudes=amplitudes, integrals=integrals, irrep_ef=irrep_ef, irrep_ab=irrep_ab)


def reference(amplitudes, integrals, irrep_ef, irrep_ab):
    def add_block(index, total):
        start = (index * EF_DEV).astype(jnp.int32)
        left = lax.dynamic_slice_in_dim(amplitudes, start, EF_DEV, 1)
        right = lax.dynamic_slice_in_dim(integrals, start, EF_DEV, 0)
        labels = lax.dynamic_slice_in_dim(irrep_ef, start, EF_DEV, 0)
        allowed = labels[:, None] == irrep_ab[None, :]
        blocked = jnp.where(allowed, right, jnp.zeros_like(right))
        return total + jnp.dot(left, blocked, preferred_element_type=jnp.float32)

    empty = jnp.zeros((OP, AB), jnp.float32)
    return lax.fori_loop(0, EF // EF_DEV, add_block, empty)
```

```python
import functools

import jax
import jax.numpy as jnp
from jax import lax
from jax.experimental import pallas as pl
from jax.experimental.pallas import tpu as pltpu
from jax.sharding import PartitionSpec as P

MESH = pl.DeviceIdType.MESH
SIDE = 4
GROUPS = 4
SLOTS = 8
HIGH = 8
CHUNKS = 4
AHEAD = 2


def kernel(
    rows, width,
    amp, integ, ef_ref, ab_ref, out_ref,
    got, blocked, acc, sib, chip, zgot, final, total,
    send_sem, recv_sem, self_sem, integ_sem,
    sib_send, sib_recv, z_send, z_recv, fin_send, fin_recv,
):
    low = rows - HIGH
    me, grp = lax.axis_index("mem"), lax.axis_index("grp")
    x, y, z = me // 8, lax.rem(me // 2, 4), lax.rem(me, 2)
    z_hi, core = grp // 2, lax.rem(grp, 2)
    piece = width // CHUNKS
    cols = integ.shape[1] // 4

    def own_copy(half):
        count = HIGH if half == 0 else low
        return pltpu.make_async_copy(
            amp.at[pl.ds(half * HIGH, count), pl.ds(pl.multiple_of(me * width, 128), width)],
            got.at[0, z, half, pl.ds(0, count)],
            self_sem.at[half],
        )

    def integ_copy(c):
        span = pl.ds(c * piece, piece)
        return pltpu.make_async_copy(integ.at[span], blocked.at[span], integ_sem.at[c])

    own_copy(0).start()
    own_copy(1).start()
    for c in range(CHUNKS):
        integ_copy(c).start()

    barrier = pltpu.get_barrier_semaphore()

    @pl.loop(1, 32)
    def _(step):
        pl.semaphore_signal(barrier, inc=1, device_id={"mem": lax.rem(me + step, 32)}, device_id_type=MESH)

    sibling = {"grp": z_hi * 2 + 1 - core}
    partner = {"grp": (1 - z_hi) * 2 + core, "mem": me + 1 - 2 * z}
    pl.semaphore_signal(barrier, inc=1, device_id=sibling, device_id_type=MESH)
    pl.semaphore_signal(barrier, inc=1, device_id=partner, device_id_type=MESH)
    pl.semaphore_wait(barrier, 33)

    def send(k, c):
        @pl.loop(0, SLOTS)
        def _(j):
            first = j // 2
            e = (1 - core) * first + core * lax.rem(SIDE - first, SIDE)
            target = lax.rem(x + e, SIDE) * 8 + lax.rem(y + e + k, SIDE) * 2 + lax.rem(j, 2)

            @pl.when(target != me)
            def _():
                span = pl.ds(pl.multiple_of(target * width + c * piece, 128), piece)
                there = pl.ds(c * piece, piece)
                for half, count in ((0, HIGH), (1, low)):
                    pltpu.make_async_remote_copy(
                        src_ref=amp.at[pl.ds(half * HIGH, count), span],
                        dst_ref=got.at[k, e * 2 + z, half, pl.ds(0, count), there],
                        send_sem=send_sem.at[k, half],
                        recv_sem=recv_sem.at[k, c, half],
                        device_id={"mem": target},
                        device_id_type=MESH,
                    ).start()

    for k in range(AHEAD):
        for c in range(CHUNKS):
            send(k, c)

    def settle(ref, sem):
        pltpu.make_async_copy(ref, ref, sem).wait()

    def mask(c):
        integ_copy(c).wait()

        @pl.loop(c * (piece // 128), (c + 1) * (piece // 128))
        def _(b):
            label = ef_ref[pl.ds(b, 1), :].astype(jnp.float32)
            column = jnp.broadcast_to(label, (128, 128)).T
            here = pl.ds(pl.multiple_of(b * 128, 128), 128)
            for n in range(integ.shape[1] // 128):
                row = ab_ref[pl.ds(n, 1), :].astype(jnp.float32)
                allowed = (column == row).astype(jnp.float32).astype(jnp.bfloat16)
                lanes = pl.ds(n * 128, 128)
                blocked[here, lanes] = blocked[here, lanes] * allowed

    def multiply(k, c):
        count = SLOTS - 1 if k == 0 else SLOTS
        there = pl.ds(c * piece, piece)
        settle(got.at[k, pl.ds(0, count), 0, :, there], recv_sem.at[k, c, 0])
        settle(got.at[k, pl.ds(0, count), 1, pl.ds(0, low), there], recv_sem.at[k, c, 1])
        left = got[k, :, :, :, there].astype(jnp.float32).reshape(SLOTS * 16, piece).astype(jnp.bfloat16)

        @pl.loop(0, 4)
        def _(g):
            right = blocked[there, pl.ds(pl.multiple_of(g * cols, 128), cols)]
            product = jnp.dot(left, right, preferred_element_type=jnp.float32)
            if c == 0:
                acc[k, g] = product
            else:
                acc[k, g] += product

    def sib_copy(k, zh):
        return pltpu.make_async_remote_copy(
            src_ref=acc.at[k, zh * 2 + 1 - core], dst_ref=sib.at[k, zh],
            send_sem=sib_send.at[k, zh], recv_sem=sib_recv.at[k, zh],
            device_id=sibling, device_id_type=MESH,
        )

    def z_copy(k):
        return pltpu.make_async_remote_copy(
            src_ref=chip.at[k, 1 - z_hi], dst_ref=zgot.at[k],
            send_sem=z_send.at[k], recv_sem=z_recv.at[k],
            device_id=partner, device_id_type=MESH,
        )

    def reduce_start(k):
        sib_copy(k, 0).start()
        sib_copy(k, 1).start()

    def reduce_mid(k):
        for zh in range(2):
            sib_copy(k, zh).wait()
            chip[k, zh] = acc[k, zh * 2 + core] + sib[k, zh]
        z_copy(k).start()

    def reduce_end(k):
        z_copy(k).wait()
        chip[k, z_hi] = chip[k, z_hi] + zgot[k]

        @pl.loop(0, SLOTS)
        def _(j):
            e = j // 2
            owner = lax.rem(x - e + SIDE, SIDE) * 8 + lax.rem(y - e - k + 2 * SIDE, SIDE) * 2 + lax.rem(j, 2)

            @pl.when(owner != me)
            def _():
                for half, count in ((0, HIGH), (1, low)):
                    pltpu.make_async_remote_copy(
                        src_ref=chip.at[k, z_hi, pl.ds(pl.multiple_of(j * 16 + half * HIGH, 8), count)],
                        dst_ref=final.at[k, e * 2 + z, half, pl.ds(0, count)],
                        send_sem=fin_send.at[k, half],
                        recv_sem=fin_recv.at[k, half],
                        device_id={"mem": owner},
                        device_id_type=MESH,
                    ).start()

            @pl.when(owner == me)
            def _():
                for half in range(2):
                    final[k, e * 2 + z, half] = chip[k, z_hi, pl.ds(pl.multiple_of(j * 16 + half * HIGH, 8), HIGH)]

    def collect(k):
        count = SLOTS - 1 if k == 0 else SLOTS
        settle(final.at[k, pl.ds(0, count), 0], fin_recv.at[k, 0])
        settle(final.at[k, pl.ds(0, count), 1, pl.ds(0, low)], fin_recv.at[k, 1])
        added = final[k, 0]
        for s in range(1, SLOTS):
            added = added + final[k, s]
        if k == 0:
            total[...] = added
        else:
            total[...] += added

    for k in range(GROUPS):
        for c in range(CHUNKS):
            if k == 0:
                mask(c)
                if c == 0:
                    own_copy(0).wait()
                    own_copy(1).wait()
            multiply(k, c)
            if k + AHEAD < GROUPS:
                send(k + AHEAD, c)
            if k > 0 and c == 0:
                reduce_mid(k - 1)
            if k > 0 and c == 2:
                reduce_end(k - 1)
        reduce_start(k)
    last = GROUPS - 1
    reduce_mid(last)
    for k in range(GROUPS):
        count = SLOTS - 1 if k == 0 else SLOTS
        settle(got.at[k, pl.ds(0, count), 0], send_sem.at[k, 0])
        settle(got.at[k, pl.ds(0, count), 1, pl.ds(0, low)], send_sem.at[k, 1])
    for k in range(last):
        collect(k)
    reduce_end(last)
    collect(last)
    for k in range(GROUPS):
        count = SLOTS - 1 if k == 0 else SLOTS
        settle(final.at[k, pl.ds(0, count), 0], fin_send.at[k, 0])
        settle(final.at[k, pl.ds(0, count), 1, pl.ds(0, low)], fin_send.at[k, 1])
    out_ref[pl.ds(0, HIGH), :] = total[0]
    out_ref[pl.ds(HIGH, low), :] = total[1, pl.ds(0, low), :]


def local(amplitudes, integrals, irrep_ef, irrep_ab):
    rows, (width, ab) = amplitudes.shape[0], integrals.shape
    cols = ab // 4
    dma, vmem = pltpu.SemaphoreType.DMA, pltpu.VMEM
    return pl.pallas_call(
        functools.partial(kernel, rows, width),
        out_shape=jax.ShapeDtypeStruct((rows, cols), jnp.float32),
        in_specs=[
            pl.BlockSpec(memory_space=pl.ANY),
            pl.BlockSpec(memory_space=pl.ANY),
            pl.BlockSpec(memory_space=vmem),
            pl.BlockSpec(memory_space=vmem),
        ],
        out_specs=pl.BlockSpec(memory_space=vmem),
        scratch_shapes=[
            vmem((GROUPS, SLOTS, 2, HIGH, width), jnp.bfloat16),
            vmem((width, ab), jnp.bfloat16),
            vmem((GROUPS, 4, SLOTS * 16, cols), jnp.float32),
            vmem((GROUPS, 2, SLOTS * 16, cols), jnp.float32),
            vmem((GROUPS, 2, SLOTS * 16, cols), jnp.float32),
            vmem((GROUPS, SLOTS * 16, cols), jnp.float32),
            vmem((GROUPS, SLOTS, 2, HIGH, cols), jnp.float32),
            vmem((2, HIGH, cols), jnp.float32),
            dma((GROUPS, 2)), dma((GROUPS, CHUNKS, 2)), dma((2,)), dma((CHUNKS,)),
            dma((GROUPS, 2)), dma((GROUPS, 2)), dma((GROUPS,)), dma((GROUPS,)),
            dma((GROUPS, 2)), dma((GROUPS, 2)),
        ],
        compiler_params=pltpu.CompilerParams(
            collective_id=0, has_side_effects=True, vmem_limit_bytes=56 * 2**20
        ),
    )(amplitudes, integrals, irrep_ef.reshape(-1, 128), irrep_ab.reshape(-1, 128))


def solution(mesh):
    placed = (P("mem", "grp"), P(("grp", "mem"), None), P(("grp", "mem")), P())
    return jax.shard_map(
        local, mesh=mesh, in_specs=placed, out_specs=P("mem", "grp"), check_vma=False
    )
```

```python
import functools

import jax
import jax.numpy as jnp
from jax import lax
from jax.experimental import pallas as pl
from jax.experimental.pallas import tpu as pltpu
from jax.sharding import PartitionSpec as P

MESH = pl.DeviceIdType.MESH
SIDE = 4
HIGH = 8
GROUPS = [[(0, 0), (2, 2), (1, 1), (3, 3)], [(0, 1), (0, 3), (2, 1), (2, 3)], [(1, 0), (3, 0), (1, 2), (3, 2)], [(0, 2), (2, 0)], [(1, 3), (3, 1)]]
PIECES = [4, 4, 4, 4, 4]
AHEAD = 6
LAG = 5
FIRST = [sum(len(g) for g in GROUPS[:k]) for k in range(len(GROUPS) + 1)]
ENTRIES = FIRST[-1]
LAST = len(GROUPS) - 1


def mirror(group, n):
    dx, dy = group[n]
    for want in ((-dx % SIDE, -dy % SIDE), (-dx % SIDE, None)):
        for m, (a, b) in enumerate(group):
            if a == want[0] and want[1] in (None, b):
                return m
    return n


def kernel(
    rows, width,
    amp, integ, ef_ref, ab_ref, out_ref,
    got, blocked, acc, sib, chip, zgot, final, direct, total,
    send_sem, recv_sem, self_sem, integ_sem, all_sem,
    sib_send, sib_recv, z_send, z_recv, fin_send, fin_recv, dir_send, dir_recv,
):
    low = rows - HIGH
    me, grp = lax.axis_index("mem"), lax.axis_index("grp")
    x, y, z = me // 8, lax.rem(me // 2, SIDE), lax.rem(me, 2)
    z_hi, core = grp // 2, lax.rem(grp, 2)
    cols = integ.shape[1] // 4
    halves = ((0, HIGH), (1, low))
    mask_pieces = 4

    def own_copy(half, count):
        return pltpu.make_async_copy(
            amp.at[pl.ds(half * HIGH, count), pl.ds(pl.multiple_of(me * width, 128), width)],
            got.at[z, half, pl.ds(0, count)],
            self_sem.at[half],
        )

    def integ_copy(c):
        span = pl.ds(c * (width // mask_pieces), width // mask_pieces)
        return pltpu.make_async_copy(integ.at[span], blocked.at[span], integ_sem.at[c])

    barrier = pltpu.get_barrier_semaphore()

    @pl.loop(1, 32)
    def _(step):
        pl.semaphore_signal(barrier, inc=1, device_id={"mem": lax.rem(me + step, 32)}, device_id_type=MESH)

    for step in range(1, 4):
        pl.semaphore_signal(barrier, inc=1, device_id={"grp": lax.rem(grp + step, 4)}, device_id_type=MESH)
    for half, count in halves:
        own_copy(half, count).start()
    for c in range(mask_pieces):
        integ_copy(c).start()
    acc[...] = jnp.zeros_like(acc)
    pl.semaphore_wait(barrier, 34)

    sibling = {"grp": z_hi * 2 + 1 - core}
    partner = {"grp": (1 - z_hi) * 2 + core, "mem": me + 1 - 2 * z}

    def pick(group, n):
        m = mirror(group, n)
        (a, b), (c, d) = group[n], group[m]
        if m == n:
            return n, a, b
        return n + core * (m - n), a + core * (c - a), b + core * (d - b)

    def send(k, c):
        piece = width // PIECES[k]
        there = pl.ds(c * piece, piece)
        group = GROUPS[k]
        for n, dz in [(n, (n + r) % 2) for r in range(2) for n in range(len(group))]:
            if group[n] == (0, 0) and dz == 0:
                continue
            place, dx, dy = pick(group, n)
            target = lax.rem(x + dx, SIDE) * 8 + lax.rem(y + dy, SIDE) * 2 + lax.rem(z + dz, 2)
            span = pl.ds(pl.multiple_of(target * width + c * piece, 128), piece)
            for half, count in halves:
                pltpu.make_async_remote_copy(
                    src_ref=amp.at[pl.ds(half * HIGH, count), span],
                    dst_ref=got.at[(FIRST[k] + place) * 2 + z, half, pl.ds(0, count), there],
                    send_sem=send_sem.at[k, half],
                    recv_sem=recv_sem.at[k, c, half],
                    device_id={"mem": target},
                    device_id_type=MESH,
                ).start()

    def settle(ref, sem):
        pltpu.make_async_copy(ref, ref, sem).wait()

    def settle_rows(ref, k, sem, *there):
        slots = pl.ds(FIRST[k] * 2, len(GROUPS[k]) * 2 - ((0, 0) in GROUPS[k]))
        for half, count in halves:
            settle(ref.at[(slots, half, pl.ds(0, count), *there)], sem(half))

    def mask(c):
        integ_copy(c).wait()
        blocks = width // mask_pieces // 128

        @pl.loop(c * blocks, (c + 1) * blocks)
        def _(b):
            label = ef_ref[pl.ds(b, 1), :].astype(jnp.float32)
            column = jnp.broadcast_to(label, (128, 128)).T
            here = pl.ds(pl.multiple_of(b * 128, 128), 128)
            for n in range(integ.shape[1] // 128):
                row = ab_ref[pl.ds(n, 1), :].astype(jnp.float32)
                allowed = (column == row).astype(jnp.float32).astype(jnp.bfloat16)
                lanes = pl.ds(n * 128, 128)
                blocked[here, lanes] = blocked[here, lanes] * allowed

    def span_of(k):
        return pl.ds(FIRST[k] * 32, len(GROUPS[k]) * 32)

    def arrive(k, c):
        piece = width // PIECES[k]
        settle_rows(got, k, lambda half: recv_sem.at[k, c, half], pl.ds(c * piece, piece))

    def multiply(k, c):
        piece = width // PIECES[k]
        deep = min(piece, 2048)

        @pl.loop(0, piece // deep)
        def _(part):
            there = pl.ds(pl.multiple_of(c * piece + part * deep, 128), deep)
            left = got[pl.ds(FIRST[k] * 2, len(GROUPS[k]) * 2), :, :, there].astype(jnp.float32)
            left = left.reshape(len(GROUPS[k]) * 32, deep).astype(jnp.bfloat16)
            product = jnp.dot(left, blocked[there, :], preferred_element_type=jnp.float32)
            for g in range(4):
                acc[g, span_of(k)] += product[:, g * cols : (g + 1) * cols]

    def sib_copy(k, zh):
        return pltpu.make_async_remote_copy(
            src_ref=acc.at[zh * 2 + 1 - core, span_of(k)], dst_ref=sib.at[zh, span_of(k)],
            send_sem=sib_send.at[k, zh], recv_sem=sib_recv.at[k, zh],
            device_id=sibling, device_id_type=MESH,
        )

    def z_copy(k):
        return pltpu.make_async_remote_copy(
            src_ref=chip.at[1 - z_hi, span_of(k)], dst_ref=zgot.at[span_of(k)],
            send_sem=z_send.at[k], recv_sem=z_recv.at[k],
            device_id=partner, device_id_type=MESH,
        )

    def reduce_start(k):
        sib_copy(k, 0).start()
        sib_copy(k, 1).start()

    def reduce_mid(k):
        for zh in range(2):
            sib_copy(k, zh).wait()
            chip[zh, span_of(k)] = acc[zh * 2 + core, span_of(k)] + sib[zh, span_of(k)]
        z_copy(k).start()

    def owner_of(k, n, zs):
        dx, dy = GROUPS[k][n]
        return lax.rem(x + SIDE - dx, SIDE) * 8 + lax.rem(y + SIDE - dy, SIDE) * 2 + zs

    def reduce_end(k):
        z_copy(k).wait()
        chip[z_hi, span_of(k)] = chip[z_hi, span_of(k)] + zgot[span_of(k)]
        for n in range(len(GROUPS[k])):
            for zs in range(2):
                owner = owner_of(k, n, zs)
                top = (FIRST[k] + n) * 32 + zs * 16

                def start(owner=owner, top=top, n=n):
                    for half, count in halves:
                        pltpu.make_async_remote_copy(
                            src_ref=chip.at[z_hi, pl.ds(top + half * HIGH, count)],
                            dst_ref=final.at[(FIRST[k] + n) * 2 + z, half, pl.ds(0, count)],
                            send_sem=fin_send.at[k, half],
                            recv_sem=fin_recv.at[k, half],
                            device_id={"mem": owner},
                            device_id_type=MESH,
                        ).start()

                def keep(top=top, n=n):
                    for half, count in halves:
                        final[(FIRST[k] + n) * 2 + z, half] = chip[z_hi, pl.ds(top + half * HIGH, HIGH)]

                if GROUPS[k][n] == (0, 0):
                    pl.when(owner != me)(start)
                    pl.when(owner == me)(keep)
                else:
                    start()

    def collect(k):
        settle_rows(final, k, lambda half: fin_recv.at[k, half])
        added = final[FIRST[k] * 2]
        for slot in range(FIRST[k] * 2 + 1, FIRST[k + 1] * 2):
            added = added + final[slot]
        total[...] = total[...] + added if k else added

    def direct_start(k):
        @pl.loop(0, 4)
        def _(g):
            for n in range(len(GROUPS[k])):
                for zs in range(2):
                    top = (FIRST[k] + n) * 32 + zs * 16
                    for half, count in halves:
                        pltpu.make_async_remote_copy(
                            src_ref=acc.at[g, pl.ds(top + half * HIGH, count)],
                            dst_ref=direct.at[n, z, grp, half, pl.ds(0, count)],
                            send_sem=dir_send.at[half],
                            recv_sem=dir_recv.at[half],
                            device_id={"grp": g, "mem": owner_of(k, n, zs)},
                            device_id_type=MESH,
                        ).start()

    def settle_direct(sem):
        for half, count in halves:
            settle(direct.at[:, :, :, half, pl.ds(0, count)], sem.at[half])

    steps = [(k, c) for k in range(LAST + 1) for c in range(PIECES[k])]
    for k, c in steps[:AHEAD]:
        send(k, c)
    for step in range(1, 4):
        pl.semaphore_signal(all_sem, inc=1, device_id={"grp": lax.rem(grp + step, 4)}, device_id_type=MESH)
    for c in range(mask_pieces):
        mask(c)
    for half, count in halves:
        own_copy(half, count).wait()
    pl.semaphore_wait(all_sem, 3)
    ends = {k: sum(PIECES[: k + 1]) - 1 for k in range(LAST)}
    for i, (k, c) in enumerate(steps):
        arrive(k, c)
        if i + AHEAD < len(steps):
            send(*steps[i + AHEAD])
        for old, end in ends.items():
            if i == end + LAG:
                reduce_mid(old)
            if i == end + 2 * LAG:
                reduce_end(old)
        multiply(k, c)
        if k < LAST and i == ends[k]:
            reduce_start(k)
    direct_start(LAST)
    for old, end in ends.items():
        if end + LAG >= len(steps):
            reduce_mid(old)
    for old, end in ends.items():
        if end + 2 * LAG >= len(steps):
            reduce_end(old)
    for k in range(LAST + 1):
        settle_rows(got, k, lambda half: send_sem.at[k, half])
    for k in range(LAST):
        collect(k)
    for k in range(LAST):
        settle_rows(final, k, lambda half: fin_send.at[k, half])
    settle_direct(dir_recv)
    for n in range(len(GROUPS[LAST])):
        for zs in range(2):
            for g in range(4):
                total[...] += direct[n, zs, g]
    out_ref[pl.ds(0, HIGH), :] = total[0]
    out_ref[pl.ds(HIGH, low), :] = total[1, pl.ds(0, low), :]
    settle_direct(dir_send)


def local(amplitudes, integrals, irrep_ef, irrep_ab):
    rows, (width, ab) = amplitudes.shape[0], integrals.shape
    cols, deep, n = ab // 4, ENTRIES * 32, LAST + 1
    dma, vmem = pltpu.SemaphoreType.DMA, pltpu.VMEM
    return pl.pallas_call(
        functools.partial(kernel, rows, width),
        out_shape=jax.ShapeDtypeStruct((rows, cols), jnp.float32),
        in_specs=[
            pl.BlockSpec(memory_space=pl.ANY),
            pl.BlockSpec(memory_space=pl.ANY),
            pl.BlockSpec(memory_space=vmem),
            pl.BlockSpec(memory_space=vmem),
        ],
        out_specs=pl.BlockSpec(memory_space=vmem),
        scratch_shapes=[
            vmem((ENTRIES * 2, 2, HIGH, width), jnp.bfloat16),
            vmem((width, ab), jnp.bfloat16),
            vmem((4, deep, cols), jnp.float32),
            vmem((2, deep, cols), jnp.float32),
            vmem((2, deep, cols), jnp.float32),
            vmem((deep, cols), jnp.float32),
            vmem((ENTRIES * 2, 2, HIGH, cols), jnp.float32),
            vmem((len(GROUPS[LAST]), 2, 4, 2, HIGH, cols), jnp.float32),
            vmem((2, HIGH, cols), jnp.float32),
            dma((n, 2)), dma((n, max(PIECES), 2)), dma((2,)), dma((4,)), pltpu.SemaphoreType.REGULAR,
            dma((n, 2)), dma((n, 2)), dma((n,)), dma((n,)),
            dma((n, 2)), dma((n, 2)), dma((2,)), dma((2,)),
        ],
        compiler_params=pltpu.CompilerParams(
            collective_id=0, has_side_effects=True, vmem_limit_bytes=56 * 2**20
        ),
    )(amplitudes, integrals, irrep_ef.reshape(-1, 128), irrep_ab.reshape(-1, 128))


def solution(mesh):
    placed = (P("mem", "grp"), P(("grp", "mem"), None), P(("grp", "mem")), P())
    return jax.shard_map(
        local, mesh=mesh, in_specs=placed, out_specs=P("mem", "grp"), check_vma=False
    )
```

```python
import functools

import jax
import jax.numpy as jnp
from jax import lax
from jax.experimental import pallas as pl
from jax.experimental.pallas import tpu as pltpu
from jax.sharding import PartitionSpec as P

MESH = pl.DeviceIdType.MESH
SIDE = 4
HIGH = 8
GROUPS = [[(0, 0), (2, 2), (1, 1), (3, 3)], [(0, 1), (0, 3), (2, 1), (2, 3)], [(1, 0), (3, 0), (1, 2), (3, 2)], [(0, 2), (2, 0)], [(1, 3), (3, 1)]]
PIECES = [4, 4, 4, 4, 4]
AHEAD = 6
LAG = 7
FIRST = [sum(len(g) for g in GROUPS[:k]) for k in range(len(GROUPS) + 1)]
ENTRIES = FIRST[-1]
LAST = len(GROUPS) - 1
DEEP = 24


def mirror(group, n):
    dx, dy = group[n]
    for want in ((-dx % SIDE, -dy % SIDE), (-dx % SIDE, None)):
        for m, (a, b) in enumerate(group):
            if a == want[0] and want[1] in (None, b):
                return m
    return n


def kernel(
    rows, width,
    amp, integ, ef_ref, ab_ref, out_ref,
    got, got_low, blocked, acc, sib, chip, zgot, final, direct, total,
    send_sem, recv_sem, self_sem, integ_sem, all_sem,
    sib_send, sib_recv, z_send, z_recv, fin_send, fin_recv, dir_send, dir_recv,
):
    low = rows - HIGH
    me, grp = lax.axis_index("mem"), lax.axis_index("grp")
    x, y, z = me // 8, lax.rem(me // 2, SIDE), lax.rem(me, 2)
    z_hi, core = grp // 2, lax.rem(grp, 2)
    cols = integ.shape[1] // 4
    halves = ((0, HIGH), (1, low))
    mask_pieces = 4

    def own_copy(half, count):
        return pltpu.make_async_copy(
            amp.at[pl.ds(half * HIGH, count), pl.ds(pl.multiple_of(me * width, 128), width)],
            got.at[z] if half == 0 else got_low.at[0, pl.ds(z * low, low)],
            self_sem.at[half],
        )

    def integ_copy(c):
        span = pl.ds(c * (width // mask_pieces), width // mask_pieces)
        return pltpu.make_async_copy(integ.at[span], blocked.at[span], integ_sem.at[c])

    barrier = pltpu.get_barrier_semaphore()

    @pl.loop(1, 32)
    def _(step):
        pl.semaphore_signal(barrier, inc=1, device_id={"mem": lax.rem(me + step, 32)}, device_id_type=MESH)

    for step in range(1, 4):
        pl.semaphore_signal(barrier, inc=1, device_id={"grp": lax.rem(grp + step, 4)}, device_id_type=MESH)
    for half, count in halves:
        own_copy(half, count).start()
    for c in range(mask_pieces):
        integ_copy(c).start()
    acc[...] = jnp.zeros_like(acc)
    pl.semaphore_wait(barrier, 34)

    sibling = {"grp": z_hi * 2 + 1 - core}
    partner = {"grp": (1 - z_hi) * 2 + core, "mem": me + 1 - 2 * z}

    def pick(group, n):
        m = mirror(group, n)
        (a, b), (c, d) = group[n], group[m]
        if m == n:
            return n, a, b
        return n + core * (m - n), a + core * (c - a), b + core * (d - b)

    def send(k, c):
        piece = width // PIECES[k]
        there = pl.ds(c * piece, piece)
        group = GROUPS[k]
        for n, dz in [(n, (n + r) % 2) for r in range(2) for n in range(len(group))]:
            if group[n] == (0, 0) and dz == 0:
                continue
            place, dx, dy = pick(group, n)
            target = lax.rem(x + dx, SIDE) * 8 + lax.rem(y + dy, SIDE) * 2 + lax.rem(z + dz, 2)
            span = pl.ds(pl.multiple_of(target * width + c * piece, 128), piece)
            for half, count in halves:
                pltpu.make_async_remote_copy(
                    src_ref=amp.at[pl.ds(half * HIGH, count), span],
                    dst_ref=got.at[(FIRST[k] + place) * 2 + z, :, there] if half == 0
                    else got_low.at[FIRST[k] + place, pl.ds(z * low, low), there],
                    send_sem=send_sem.at[k, half],
                    recv_sem=recv_sem.at[k, c, half],
                    device_id={"mem": target},
                    device_id_type=MESH,
                ).start()

    def settle(ref, sem):
        pltpu.make_async_copy(ref, ref, sem).wait()

    def settle_rows(ref, k, sem):
        slots = pl.ds(FIRST[k] * 2, len(GROUPS[k]) * 2 - ((0, 0) in GROUPS[k]))
        for half, count in halves:
            settle(ref.at[slots, half, pl.ds(0, count)], sem(half))

    def mask(c):
        integ_copy(c).wait()
        blocks = width // mask_pieces // 128

        @pl.loop(c * blocks, (c + 1) * blocks)
        def _(b):
            label = ef_ref[pl.ds(b, 1), :].astype(jnp.float32)
            column = jnp.broadcast_to(label, (128, 128)).T
            here = pl.ds(pl.multiple_of(b * 128, 128), 128)
            for n in range(integ.shape[1] // 128):
                row = ab_ref[pl.ds(n, 1), :].astype(jnp.float32)
                allowed = (column == row).astype(jnp.float32).astype(jnp.bfloat16)
                lanes = pl.ds(n * 128, 128)
                blocked[here, lanes] = blocked[here, lanes] * allowed

    def span_of(k):
        return pl.ds(FIRST[k] * DEEP, len(GROUPS[k]) * DEEP)

    def settle_got(k, sem, there):
        slots = pl.ds(FIRST[k] * 2, len(GROUPS[k]) * 2 - ((0, 0) in GROUPS[k]))
        settle(got.at[slots, :, there], sem(0))
        settle(got.at[slots, pl.ds(0, low), there], sem(1))

    def arrive(k, c):
        piece = width // PIECES[k]
        settle_got(k, lambda half: recv_sem.at[k, c, half], pl.ds(c * piece, piece))

    def multiply(k, c):
        piece = width // PIECES[k]
        deep = min(piece, 2048)

        @pl.loop(0, piece // deep)
        def _(part):
            there = pl.ds(pl.multiple_of(c * piece + part * deep, 128), deep)
            left = jnp.concatenate([
                got[pl.ds(FIRST[k] * 2, len(GROUPS[k]) * 2), :, there].astype(jnp.float32).reshape(-1, deep),
                got_low[pl.ds(FIRST[k], len(GROUPS[k])), :, there].astype(jnp.float32).reshape(-1, deep),
            ]).astype(jnp.bfloat16)
            product = jnp.dot(left, blocked[there, :], preferred_element_type=jnp.float32)
            for g in range(4):
                acc[g, span_of(k)] += product[:, g * cols : (g + 1) * cols]

    def sib_copy(k, zh):
        return pltpu.make_async_remote_copy(
            src_ref=acc.at[zh * 2 + 1 - core, span_of(k)], dst_ref=sib.at[zh, span_of(k)],
            send_sem=sib_send.at[k, zh], recv_sem=sib_recv.at[k, zh],
            device_id=sibling, device_id_type=MESH,
        )

    def z_copy(k):
        return pltpu.make_async_remote_copy(
            src_ref=chip.at[1 - z_hi, span_of(k)], dst_ref=zgot.at[span_of(k)],
            send_sem=z_send.at[k], recv_sem=z_recv.at[k],
            device_id=partner, device_id_type=MESH,
        )

    def reduce_start(k):
        sib_copy(k, 0).start()
        sib_copy(k, 1).start()

    def reduce_mid(k):
        for zh in range(2):
            sib_copy(k, zh).wait()
            chip[zh, span_of(k)] = acc[zh * 2 + core, span_of(k)] + sib[zh, span_of(k)]
        z_copy(k).start()

    def top_of(k, n, zs, half):
        if half == 0:
            return FIRST[k] * DEEP + (n * 2 + zs) * HIGH
        return FIRST[k] * DEEP + len(GROUPS[k]) * 2 * HIGH + n * HIGH + zs * low

    def owner_of(k, n, zs):
        dx, dy = GROUPS[k][n]
        return lax.rem(x + SIDE - dx, SIDE) * 8 + lax.rem(y + SIDE - dy, SIDE) * 2 + zs

    def reduce_end(k):
        z_copy(k).wait()
        chip[z_hi, span_of(k)] = chip[z_hi, span_of(k)] + zgot[span_of(k)]
        for n in range(len(GROUPS[k])):
            for zs in range(2):
                owner = owner_of(k, n, zs)

                def start(owner=owner, n=n, zs=zs):
                    for half, count in halves:
                        pltpu.make_async_remote_copy(
                            src_ref=chip.at[z_hi, pl.ds(top_of(k, n, zs, half), count)],
                            dst_ref=final.at[(FIRST[k] + n) * 2 + z, half, pl.ds(0, count)],
                            send_sem=fin_send.at[k, half],
                            recv_sem=fin_recv.at[k, half],
                            device_id={"mem": owner},
                            device_id_type=MESH,
                        ).start()

                def keep(n=n, zs=zs):
                    for half, count in halves:
                        mine = chip[z_hi, pl.ds(top_of(k, n, zs, half), count)]
                        final[(FIRST[k] + n) * 2 + z, half, pl.ds(0, count)] = mine

                if GROUPS[k][n] == (0, 0):
                    pl.when(owner != me)(start)
                    pl.when(owner == me)(keep)
                else:
                    start()

    def collect(k):
        settle_rows(final, k, lambda half: fin_recv.at[k, half])
        added = final[FIRST[k] * 2]
        for slot in range(FIRST[k] * 2 + 1, FIRST[k + 1] * 2):
            added = added + final[slot]
        total[...] = total[...] + added if k else added

    def direct_start(k):
        @pl.loop(0, 4)
        def _(g):
            for n in range(len(GROUPS[k])):
                for zs in range(2):
                    for half, count in halves:
                        pltpu.make_async_remote_copy(
                            src_ref=acc.at[g, pl.ds(top_of(k, n, zs, half), count)],
                            dst_ref=direct.at[n, z, grp, half, pl.ds(0, count)],
                            send_sem=dir_send.at[half],
                            recv_sem=dir_recv.at[half],
                            device_id={"grp": g, "mem": owner_of(k, n, zs)},
                            device_id_type=MESH,
                        ).start()

    def settle_direct(sem):
        for half, count in halves:
            settle(direct.at[:, :, :, half, pl.ds(0, count)], sem.at[half])

    steps = [(k, c) for k in range(LAST + 1) for c in range(PIECES[k])]
    for k, c in steps[:AHEAD]:
        send(k, c)
    for step in range(1, 4):
        pl.semaphore_signal(all_sem, inc=1, device_id={"grp": lax.rem(grp + step, 4)}, device_id_type=MESH)
    for c in range(mask_pieces):
        mask(c)
    for half, count in halves:
        own_copy(half, count).wait()
    pl.semaphore_wait(all_sem, 3)
    ends = {k: sum(PIECES[: k + 1]) - 1 for k in range(LAST)}
    for i, (k, c) in enumerate(steps):
        arrive(k, c)
        if i + AHEAD < len(steps):
            send(*steps[i + AHEAD])
        for old, end in ends.items():
            if i == end + LAG:
                reduce_mid(old)
            if i == end + 2 * LAG:
                reduce_end(old)
        multiply(k, c)
        if k < LAST and i == ends[k]:
            reduce_start(k)
    direct_start(LAST)
    for old, end in ends.items():
        if end + LAG >= len(steps):
            reduce_mid(old)
    for old, end in ends.items():
        if end + 2 * LAG >= len(steps):
            reduce_end(old)
    for k in range(LAST + 1):
        settle_got(k, lambda half: send_sem.at[k, half], pl.ds(0, width))
    for k in range(LAST):
        collect(k)
    for k in range(LAST):
        settle_rows(final, k, lambda half: fin_send.at[k, half])
    settle_direct(dir_recv)
    for n in range(len(GROUPS[LAST])):
        for zs in range(2):
            for g in range(4):
                total[...] += direct[n, zs, g]
    out_ref[pl.ds(0, HIGH), :] = total[0]
    out_ref[pl.ds(HIGH, low), :] = total[1, pl.ds(0, low), :]
    settle_direct(dir_send)


def local(amplitudes, integrals, irrep_ef, irrep_ab):
    rows, (width, ab) = amplitudes.shape[0], integrals.shape
    cols, deep, n = ab // 4, ENTRIES * DEEP, LAST + 1
    dma, vmem = pltpu.SemaphoreType.DMA, pltpu.VMEM
    return pl.pallas_call(
        functools.partial(kernel, rows, width),
        out_shape=jax.ShapeDtypeStruct((rows, cols), jnp.float32),
        in_specs=[
            pl.BlockSpec(memory_space=pl.ANY),
            pl.BlockSpec(memory_space=pl.ANY),
            pl.BlockSpec(memory_space=vmem),
            pl.BlockSpec(memory_space=vmem),
        ],
        out_specs=pl.BlockSpec(memory_space=vmem),
        scratch_shapes=[
            vmem((ENTRIES * 2, HIGH, width), jnp.bfloat16),
            vmem((ENTRIES, HIGH, width), jnp.bfloat16),
            vmem((width, ab), jnp.bfloat16),
            vmem((4, deep, cols), jnp.float32),
            vmem((2, deep, cols), jnp.float32),
            vmem((2, deep, cols), jnp.float32),
            vmem((deep, cols), jnp.float32),
            vmem((ENTRIES * 2, 2, HIGH, cols), jnp.float32),
            vmem((len(GROUPS[LAST]), 2, 4, 2, HIGH, cols), jnp.float32),
            vmem((2, HIGH, cols), jnp.float32),
            dma((n, 2)), dma((n, max(PIECES), 2)), dma((2,)), dma((4,)), pltpu.SemaphoreType.REGULAR,
            dma((n, 2)), dma((n, 2)), dma((n,)), dma((n,)),
            dma((n, 2)), dma((n, 2)), dma((2,)), dma((2,)),
        ],
        compiler_params=pltpu.CompilerParams(
            collective_id=0, has_side_effects=True, vmem_limit_bytes=56 * 2**20
        ),
    )(amplitudes, integrals, irrep_ef.reshape(-1, 128), irrep_ab.reshape(-1, 128))


def solution(mesh):
    placed = (P("mem", "grp"), P(("grp", "mem"), None), P(("grp", "mem")), P())
    return jax.shard_map(
        local, mesh=mesh, in_specs=placed, out_specs=P("mem", "grp"), check_vma=False
    )
```

```python
import functools

import jax
import jax.numpy as jnp
from jax import lax
from jax.experimental import pallas as pl
from jax.experimental.pallas import tpu as pltpu
from jax.sharding import PartitionSpec as P

MESH = pl.DeviceIdType.MESH
SIDE = 4
HIGH = 8
GROUPS = [[(0, 0), (2, 2), (1, 1), (3, 3)], [(0, 1), (0, 3), (2, 1), (2, 3)], [(1, 0), (3, 0), (1, 2), (3, 2)], [(0, 2), (2, 0)], [(1, 3), (3, 1)]]
PIECES = [4, 4, 4, 4, 4]
AHEAD = 6
LAG = 8
FIRST = [sum(len(g) for g in GROUPS[:k]) for k in range(len(GROUPS) + 1)]
ENTRIES = FIRST[-1]
LAST = len(GROUPS) - 1
DEEP = 24


def mirror(group, n):
    dx, dy = group[n]
    for want in ((-dx % SIDE, -dy % SIDE), (-dx % SIDE, None)):
        for m, (a, b) in enumerate(group):
            if a == want[0] and want[1] in (None, b):
                return m
    return n


def kernel(
    rows, width,
    amp, integ, ef_ref, ab_ref, out_ref,
    got, got_low, blocked, acc, sib, chip, zgot, final, direct, total,
    send_sem, recv_sem, self_sem, integ_sem, all_sem,
    sib_send, sib_recv, z_send, z_recv, fin_send, fin_recv, dir_send, dir_recv,
):
    low = rows - HIGH
    me, grp = lax.axis_index("mem"), lax.axis_index("grp")
    x, y, z = me // 8, lax.rem(me // 2, SIDE), lax.rem(me, 2)
    z_hi, core = grp // 2, lax.rem(grp, 2)
    cols = integ.shape[1] // 4
    halves = ((0, HIGH), (1, low))
    mask_pieces = 4

    def own_copy(half, count):
        return pltpu.make_async_copy(
            amp.at[pl.ds(half * HIGH, count), pl.ds(pl.multiple_of(me * width, 128), width)],
            got.at[z] if half == 0 else got_low.at[0, pl.ds(z * low, low)],
            self_sem.at[half],
        )

    def integ_copy(c):
        span = pl.ds(c * (width // mask_pieces), width // mask_pieces)
        return pltpu.make_async_copy(integ.at[span], blocked.at[span], integ_sem.at[c])

    barrier = pltpu.get_barrier_semaphore()

    @pl.loop(1, 32)
    def _(step):
        pl.semaphore_signal(barrier, inc=1, device_id={"mem": lax.rem(me + step, 32)}, device_id_type=MESH)

    for step in range(1, 4):
        pl.semaphore_signal(barrier, inc=1, device_id={"grp": lax.rem(grp + step, 4)}, device_id_type=MESH)
    for half, count in halves:
        own_copy(half, count).start()
    for c in range(mask_pieces):
        integ_copy(c).start()
    acc[...] = jnp.zeros_like(acc)
    pl.semaphore_wait(barrier, 34)

    sibling = {"grp": z_hi * 2 + 1 - core}
    partner = {"grp": (1 - z_hi) * 2 + core, "mem": me + 1 - 2 * z}

    def pick(group, n):
        m = mirror(group, n)
        (a, b), (c, d) = group[n], group[m]
        if m == n:
            return n, a, b
        return n + core * (m - n), a + core * (c - a), b + core * (d - b)

    def send(k, c):
        piece = width // PIECES[k]
        there = pl.ds(c * piece, piece)
        group = GROUPS[k]
        for n, dz in [(n, (n + r + c) % 2) for r in range(2) for n in range(len(group))]:
            if group[n] == (0, 0) and dz == 0:
                continue
            place, dx, dy = pick(group, n)
            target = lax.rem(x + dx, SIDE) * 8 + lax.rem(y + dy, SIDE) * 2 + lax.rem(z + dz, 2)
            span = pl.ds(pl.multiple_of(target * width + c * piece, 128), piece)
            for half, count in halves:
                pltpu.make_async_remote_copy(
                    src_ref=amp.at[pl.ds(half * HIGH, count), span],
                    dst_ref=got.at[(FIRST[k] + place) * 2 + z, :, there] if half == 0
                    else got_low.at[FIRST[k] + place, pl.ds(z * low, low), there],
                    send_sem=send_sem.at[k, half],
                    recv_sem=recv_sem.at[k, c, half],
                    device_id={"mem": target},
                    device_id_type=MESH,
                ).start()

    def settle(ref, sem):
        pltpu.make_async_copy(ref, ref, sem).wait()

    def settle_rows(ref, k, sem):
        slots = pl.ds(FIRST[k] * 2, len(GROUPS[k]) * 2 - ((0, 0) in GROUPS[k]))
        for half, count in halves:
            settle(ref.at[slots, half, pl.ds(0, count)], sem(half))

    def mask(c):
        integ_copy(c).wait()
        blocks = width // mask_pieces // 128

        @pl.loop(c * blocks, (c + 1) * blocks)
        def _(b):
            label = ef_ref[pl.ds(b, 1), :].astype(jnp.float32)
            column = jnp.broadcast_to(label, (128, 128)).T
            here = pl.ds(pl.multiple_of(b * 128, 128), 128)
            for n in range(integ.shape[1] // 128):
                row = ab_ref[pl.ds(n, 1), :].astype(jnp.float32)
                allowed = (column == row).astype(jnp.float32).astype(jnp.bfloat16)
                lanes = pl.ds(n * 128, 128)
                blocked[here, lanes] = blocked[here, lanes] * allowed

    def span_of(k):
        return pl.ds(FIRST[k] * DEEP, len(GROUPS[k]) * DEEP)

    def settle_got(k, sem, there):
        slots = pl.ds(FIRST[k] * 2, len(GROUPS[k]) * 2 - ((0, 0) in GROUPS[k]))
        settle(got.at[slots, :, there], sem(0))
        settle(got.at[slots, pl.ds(0, low), there], sem(1))

    def arrive(k, c):
        piece = width // PIECES[k]
        settle_got(k, lambda half: recv_sem.at[k, c, half], pl.ds(c * piece, piece))

    def multiply(k, c):
        piece = width // PIECES[k]
        deep = min(piece, 2048)

        @pl.loop(0, piece // deep)
        def _(part):
            there = pl.ds(pl.multiple_of(c * piece + part * deep, 128), deep)
            left = jnp.concatenate([
                got[pl.ds(FIRST[k] * 2, len(GROUPS[k]) * 2), :, there].astype(jnp.float32).reshape(-1, deep),
                got_low[pl.ds(FIRST[k], len(GROUPS[k])), :, there].astype(jnp.float32).reshape(-1, deep),
            ]).astype(jnp.bfloat16)
            product = jnp.dot(left, blocked[there, :], preferred_element_type=jnp.float32)
            for g in range(4):
                acc[g, span_of(k)] += product[:, g * cols : (g + 1) * cols]

    def sib_copy(k, zh):
        return pltpu.make_async_remote_copy(
            src_ref=acc.at[zh * 2 + 1 - core, span_of(k)], dst_ref=sib.at[zh, span_of(k)],
            send_sem=sib_send.at[k, zh], recv_sem=sib_recv.at[k, zh],
            device_id=sibling, device_id_type=MESH,
        )

    def z_copy(k):
        return pltpu.make_async_remote_copy(
            src_ref=chip.at[1 - z_hi, span_of(k)], dst_ref=zgot.at[span_of(k)],
            send_sem=z_send.at[k], recv_sem=z_recv.at[k],
            device_id=partner, device_id_type=MESH,
        )

    def reduce_start(k):
        sib_copy(k, 0).start()
        sib_copy(k, 1).start()

    def reduce_mid(k):
        for zh in range(2):
            sib_copy(k, zh).wait()
            chip[zh, span_of(k)] = acc[zh * 2 + core, span_of(k)] + sib[zh, span_of(k)]
        z_copy(k).start()

    def top_of(k, n, zs, half):
        if half == 0:
            return FIRST[k] * DEEP + (n * 2 + zs) * HIGH
        return FIRST[k] * DEEP + len(GROUPS[k]) * 2 * HIGH + n * HIGH + zs * low

    def owner_of(k, n, zs):
        dx, dy = GROUPS[k][n]
        return lax.rem(x + SIDE - dx, SIDE) * 8 + lax.rem(y + SIDE - dy, SIDE) * 2 + zs

    def reduce_end(k):
        z_copy(k).wait()
        chip[z_hi, span_of(k)] = chip[z_hi, span_of(k)] + zgot[span_of(k)]
        for n in range(len(GROUPS[k])):
            for zs in range(2):
                owner = owner_of(k, n, zs)

                def start(owner=owner, n=n, zs=zs):
                    for half, count in halves:
                        pltpu.make_async_remote_copy(
                            src_ref=chip.at[z_hi, pl.ds(top_of(k, n, zs, half), count)],
                            dst_ref=final.at[(FIRST[k] + n) * 2 + z, half, pl.ds(0, count)],
                            send_sem=fin_send.at[k, half],
                            recv_sem=fin_recv.at[k, half],
                            device_id={"mem": owner},
                            device_id_type=MESH,
                        ).start()

                def keep(n=n, zs=zs):
                    for half, count in halves:
                        mine = chip[z_hi, pl.ds(top_of(k, n, zs, half), count)]
                        final[(FIRST[k] + n) * 2 + z, half, pl.ds(0, count)] = mine

                if GROUPS[k][n] == (0, 0):
                    pl.when(owner != me)(start)
                    pl.when(owner == me)(keep)
                else:
                    start()

    def collect(k):
        settle_rows(final, k, lambda half: fin_recv.at[k, half])
        added = final[FIRST[k] * 2]
        for slot in range(FIRST[k] * 2 + 1, FIRST[k + 1] * 2):
            added = added + final[slot]
        total[...] = total[...] + added if k else added

    def direct_start(k):
        @pl.loop(0, 4)
        def _(g):
            for n in range(len(GROUPS[k])):
                for zs in range(2):
                    for half, count in halves:
                        pltpu.make_async_remote_copy(
                            src_ref=acc.at[g, pl.ds(top_of(k, n, zs, half), count)],
                            dst_ref=direct.at[n, z, grp, half, pl.ds(0, count)],
                            send_sem=dir_send.at[half],
                            recv_sem=dir_recv.at[half],
                            device_id={"grp": g, "mem": owner_of(k, n, zs)},
                            device_id_type=MESH,
                        ).start()

    def settle_direct(sem):
        for half, count in halves:
            settle(direct.at[:, :, :, half, pl.ds(0, count)], sem.at[half])

    steps = [(k, c) for k in range(LAST + 1) for c in range(PIECES[k])]
    for k, c in steps[:AHEAD]:
        send(k, c)
    for step in range(1, 4):
        pl.semaphore_signal(all_sem, inc=1, device_id={"grp": lax.rem(grp + step, 4)}, device_id_type=MESH)
    for c in range(mask_pieces):
        mask(c)
    for half, count in halves:
        own_copy(half, count).wait()
    pl.semaphore_wait(all_sem, 3)
    ends = {k: sum(PIECES[: k + 1]) - 1 for k in range(LAST)}
    for i, (k, c) in enumerate(steps):
        arrive(k, c)
        if i + AHEAD < len(steps):
            send(*steps[i + AHEAD])
        for old, end in ends.items():
            if i == end + LAG:
                reduce_mid(old)
            if i == end + 2 * LAG:
                reduce_end(old)
        multiply(k, c)
        if k < LAST and i == ends[k]:
            reduce_start(k)
    direct_start(LAST)
    for old, end in ends.items():
        if end + LAG >= len(steps):
            reduce_mid(old)
    for old, end in ends.items():
        if end + 2 * LAG >= len(steps):
            reduce_end(old)
    for k in range(LAST + 1):
        settle_got(k, lambda half: send_sem.at[k, half], pl.ds(0, width))
    for k in range(LAST):
        collect(k)
    for k in range(LAST):
        settle_rows(final, k, lambda half: fin_send.at[k, half])
    settle_direct(dir_recv)
    for n in range(len(GROUPS[LAST])):
        for zs in range(2):
            for g in range(4):
                total[...] += direct[n, zs, g]
    out_ref[pl.ds(0, HIGH), :] = total[0]
    out_ref[pl.ds(HIGH, low), :] = total[1, pl.ds(0, low), :]
    settle_direct(dir_send)


def local(amplitudes, integrals, irrep_ef, irrep_ab):
    rows, (width, ab) = amplitudes.shape[0], integrals.shape
    cols, deep, n = ab // 4, ENTRIES * DEEP, LAST + 1
    dma, vmem = pltpu.SemaphoreType.DMA, pltpu.VMEM
    return pl.pallas_call(
        functools.partial(kernel, rows, width),
        out_shape=jax.ShapeDtypeStruct((rows, cols), jnp.float32),
        in_specs=[
            pl.BlockSpec(memory_space=pl.ANY),
            pl.BlockSpec(memory_space=pl.ANY),
            pl.BlockSpec(memory_space=vmem),
            pl.BlockSpec(memory_space=vmem),
        ],
        out_specs=pl.BlockSpec(memory_space=vmem),
        scratch_shapes=[
            vmem((ENTRIES * 2, HIGH, width), jnp.bfloat16),
            vmem((ENTRIES, HIGH, width), jnp.bfloat16),
            vmem((width, ab), jnp.bfloat16),
            vmem((4, deep, cols), jnp.float32),
            vmem((2, deep, cols), jnp.float32),
            vmem((2, deep, cols), jnp.float32),
            vmem((deep, cols), jnp.float32),
            vmem((ENTRIES * 2, 2, HIGH, cols), jnp.float32),
            vmem((len(GROUPS[LAST]), 2, 4, 2, HIGH, cols), jnp.float32),
            vmem((2, HIGH, cols), jnp.float32),
            dma((n, 2)), dma((n, max(PIECES), 2)), dma((2,)), dma((4,)), pltpu.SemaphoreType.REGULAR,
            dma((n, 2)), dma((n, 2)), dma((n,)), dma((n,)),
            dma((n, 2)), dma((n, 2)), dma((2,)), dma((2,)),
        ],
        compiler_params=pltpu.CompilerParams(
            collective_id=0, has_side_effects=True, vmem_limit_bytes=56 * 2**20
        ),
    )(amplitudes, integrals, irrep_ef.reshape(-1, 128), irrep_ab.reshape(-1, 128))


def solution(mesh):
    placed = (P("mem", "grp"), P(("grp", "mem"), None), P(("grp", "mem")), P())
    return jax.shard_map(
        local, mesh=mesh, in_specs=placed, out_specs=P("mem", "grp"), check_vma=False
    )
```
